32 devices in a mesh: row: 4 (over y, x), col: 8 (over z, core).
Axes of the slice: x: 2, y: 2, z: 4, core: 2. Of those that a mesh axis runs over, the one named last changes fastest.
Arguments:
- potential_temp: bfloat16 [64, 1024, 1024], P(None, 'col', 'row'), may hold values from -6 to 6
- humidity: bfloat16 [64, 1024, 1024], P(None, 'col', 'row'), may hold values from 0.099609375 to 1
- absorb: float32 [4, 64], replicated, may hold values from 0.002 to 0.2
- solar_flux: float32 [4], replicated, may hold values from 2 to 8
- emission: float32 [4], replicated, may hold values from 0.5 to 4
- sunlit: int32 [4, 8], replicated, may hold values from 0 to 32768
- project: float32 [32, 64], replicated, may hold values from -0.75 to 0.75
- restore: float32 [64, 32], replicated, may hold values from -1 to 1
- east_basis: bfloat16 [1024, 1024], replicated, may hold values from -0.1875 to 0.1875
- north_basis: bfloat16 [1024, 1024], replicated, may hold values from -0.1875 to 0.1875
- east_weight: float32 [1024], replicated, may hold values from 0.5 to 2
- north_weight: float32 [1024], replicated, may hold values from 0.5 to 2
- east_eigen: float32 [1024], replicated, may hold values from 0.05 to 4
- north_eigen: float32 [1024], replicated, may hold values from 0.05 to 4
- coupling: float32 [32], replicated, may hold values from 0.05 to 2
Outputs:
- new_state: bfloat16 [64, 1024, 1024], P(None, 'col', 'row')
The draws below stay inside these ranges and needn't reach their ends.
All inputs are finite; a program needn't handle non-finite values.
Results may differ from the reference program's by a relative error of at most 0.01.
Values may be sent and summed in bfloat16 or wider, within the bound.
A program may use at most 128 MiB of HBM per device.

```python
import math
import jax
import jax.numpy as jnp
from jax import lax

NX = 1024
NY = 1024
L = 64
M = 32
BANDS = 4
TILE = 32768
N_ROW = 4
N_COL = 8


def place_ends(entries, stream_key, low, high):
    index_at = [jax.random.randint(jax.random.fold_in(stream_key, axis), (), 0, length) for axis, length in enumerate(entries.shape)]
    main_axis = entries.shape.index(max(entries.shape))
    next_to = index_at[:main_axis] + [(index_at[main_axis] + 1) % entries.shape[main_axis]] + index_at[main_axis + 1:]
    return entries.at[tuple(index_at)].set(low).at[tuple(next_to)].set(high)


def block_levels(stream_key, dims, split, smallest, top_value):
    def one(position, blocks):
        draws = jax.random.uniform(jax.random.fold_in(jax.random.fold_in(stream_key, 6), position), (blocks,), jnp.float32, smallest / len(split), top_value / len(split))
        return jnp.repeat(jnp.exp(draws), dims[position] // blocks).reshape((-1,) + (1,) * (len(dims) - position - 1))

    loudness = one(*split[0])
    for cut in split[1:]:
        loudness = loudness * one(*cut)
    return loudness


def centred(rng, extent, width, most, split=(), held_as=jnp.bfloat16):
    factor_of = block_levels(rng, extent, split, -0.22, 0.18) if split else 1.0
    result = jax.random.normal(rng, extent, jnp.float32) * width * factor_of
    return jnp.minimum(jnp.maximum(result, -most), most).astype(held_as)


def setup_inputs(seed: int = 0) -> dict:
    streams_of = jax.random.split(jax.random.key(seed), 16)
    return {
        "potential_temp": centred(streams_of[0], (L, NX, NY), 1.0, 6.0, ((1, 8), (2, 4))),
        "humidity": jnp.clip(0.099609375 + 0.9003906 * jax.random.uniform(streams_of[1], (L, NX, NY), jnp.float32) ** block_levels(streams_of[1], (L, NX, NY), ((1, 8), (2, 4)), -0.2, 0.2), 0.099609375, 1.0).astype(jnp.bfloat16),
        "absorb": jnp.clip(jnp.exp(jax.random.uniform(streams_of[2], (BANDS, L), jnp.float32, math.log(0.002), math.log(0.2))), 0.002, 0.2),
        "solar_flux": jnp.clip(jnp.exp(jax.random.uniform(streams_of[3], (BANDS,), jnp.float32, math.log(2.0), math.log(8.0))), 2.0, 8.0),
        "emission": jnp.clip(jnp.exp(jax.random.uniform(streams_of[4], (BANDS,), jnp.float32, math.log(0.5), math.log(4.0))), 0.5, 4.0),
        "sunlit": place_ends(jax.random.randint(streams_of[5], (N_ROW, N_COL), 0, TILE + 1), jax.random.fold_in(streams_of[5], 1), 0, TILE).astype(jnp.int32),
        "project": centred(streams_of[6], (M, L), L ** -0.5, 0.75, (), jnp.float32),
        "restore": centred(streams_of[7], (L, M), M ** -0.5, 1.0, (), jnp.float32),
        "east_basis": centred(streams_of[8], (NX, NX), NX ** -0.5, 0.1875),
        "north_basis": centred(streams_of[9], (NY, NY), NY ** -0.5, 0.1875),
        "east_weight": jnp.clip(jnp.exp(jax.random.uniform(streams_of[10], (NX,), jnp.float32, math.log(0.5), math.log(2.0))), 0.5, 2.0),
        "north_weight": jnp.clip(jnp.exp(jax.random.uniform(streams_of[11], (NY,), jnp.float32, math.log(0.5), math.log(2.0))), 0.5, 2.0),
        "east_eigen": jnp.clip(jnp.exp(jax.random.uniform(streams_of[12], (NX,), jnp.float32, math.log(0.05), math.log(4.0))), 0.05, 4.0),
        "north_eigen": jnp.clip(jnp.exp(jax.random.uniform(streams_of[13], (NY,), jnp.float32, math.log(0.05), math.log(4.0))), 0.05, 4.0),
        "coupling": jnp.clip(jnp.exp(jax.random.uniform(streams_of[14], (M,), jnp.float32, math.log(0.05), math.log(2.0))), 0.05, 2.0),
    }


def lower_triangle(levels):
    level_index = jnp.arange(levels, dtype=jnp.int32)
    return (level_index[:, None] >= level_index[None, :]).astype(jnp.float32)


def shortwave(vapour, absorb, solar_flux, triangle):
    heating = jnp.zeros(vapour.shape, jnp.float32)
    for band_index in range(absorb.shape[0]):
        optical = absorb[band_index][:, None] * vapour
        column_depth = jnp.dot(triangle, optical, precision=lax.Precision.HIGHEST, preferred_element_type=jnp.float32)
        heating = heating + solar_flux[band_index] * (jnp.exp(optical - column_depth) - jnp.exp(-column_depth))
    return heating


def longwave(column_temp, vapour, absorb, emission):
    cooling = jnp.zeros(vapour.shape, jnp.float32)
    for band_index in range(absorb.shape[0]):
        optical = absorb[band_index][:, None] * vapour
        cooling = cooling + emission[band_index] * (1.0 - jnp.exp(-optical)) * column_temp
    return cooling


def reference(potential_temp, humidity, absorb, solar_flux, emission, sunlit, project, restore, east_basis, north_basis, east_weight, north_weight, east_eigen, north_eigen, coupling):
    east_local = NX // N_COL
    north_local = NY // N_ROW
    east_index = jnp.arange(NX, dtype=jnp.int32)
    north_index = jnp.arange(NY, dtype=jnp.int32)
    within = (east_index % east_local)[:, None] * north_local + (north_index % north_local)[None, :]
    lit_count = sunlit[(north_index // north_local)[None, :], (east_index // east_local)[:, None]]
    mask = (within < lit_count).astype(jnp.float32).reshape(1, NX * NY)
    column_temp = potential_temp.astype(jnp.float32).reshape(L, NX * NY)
    vapour = humidity.astype(jnp.float32).reshape(L, NX * NY)
    triangle = lower_triangle(L)
    forcing = column_temp + shortwave(vapour, absorb, solar_flux, triangle) * mask - longwave(column_temp, vapour, absorb, emission)
    modal_field = jnp.dot(project, forcing, precision=lax.Precision.HIGHEST, preferred_element_type=jnp.float32).astype(jnp.bfloat16)
    modal_field = modal_field.reshape(M, NX, NY)
    east_scaled = (east_basis.astype(jnp.float32) * east_weight[:, None]).astype(jnp.bfloat16)
    north_scaled = (north_basis.astype(jnp.float32) * north_weight[:, None]).astype(jnp.bfloat16)
    spectral_east = jnp.einsum("xi,mxy->miy", east_scaled.astype(jnp.float32), modal_field.astype(jnp.float32), precision=lax.Precision.HIGHEST).astype(jnp.bfloat16)
    spectral = jnp.einsum("miy,yj->mij", spectral_east.astype(jnp.float32), north_scaled.astype(jnp.float32), precision=lax.Precision.HIGHEST)
    divisor = 1.0 + coupling[:, None, None] * (east_eigen[:, None] + north_eigen[None, :])[None]
    scaled = (spectral / divisor).astype(jnp.bfloat16)
    north_back = jnp.einsum("mij,yj->miy", scaled.astype(jnp.float32), north_basis.astype(jnp.float32), precision=lax.Precision.HIGHEST).astype(jnp.bfloat16)
    solved = jnp.einsum("xi,miy->mxy", east_basis.astype(jnp.float32), north_back.astype(jnp.float32), precision=lax.Precision.HIGHEST).astype(jnp.bfloat16)
    difference = solved.reshape(M, NX * NY).astype(jnp.float32) - modal_field.reshape(M, NX * NY).astype(jnp.float32)
    correction = jnp.dot(restore, difference, precision=lax.Precision.HIGHEST, preferred_element_type=jnp.float32)
    return (forcing + correction).astype(jnp.bfloat16).reshape(L, NX, NY)
```

```python
import functools
import math

import jax
import jax.numpy as jnp
from jax import lax
from jax.experimental import pallas as pl
from jax.experimental.pallas import tpu as pltpu
from jax.sharding import PartitionSpec as P

SUB = 8
PAIR = 16
MESH = pl.DeviceIdType.MESH
F32 = jnp.float32
BF16 = jnp.bfloat16


def spread(matrix):
    rows, cols = matrix.shape
    tall = (
        lax.broadcasted_iota(jnp.int32, (rows * SUB, rows), 0) // SUB
        == lax.broadcasted_iota(jnp.int32, (rows * SUB, rows), 1)
    ).astype(F32).astype(BF16)
    wide = (
        lax.broadcasted_iota(jnp.int32, (cols, cols * SUB), 1) // SUB
        == lax.broadcasted_iota(jnp.int32, (cols, cols * SUB), 0)
    ).astype(F32).astype(BF16)
    half = jnp.dot(tall, matrix.astype(BF16), preferred_element_type=F32).astype(BF16)
    full = jnp.dot(half, wide, preferred_element_type=F32)
    shape = (rows * SUB, cols * SUB)
    keep = (
        lax.broadcasted_iota(jnp.int32, shape, 0) % SUB
        == lax.broadcasted_iota(jnp.int32, shape, 1) % SUB
    )
    return jnp.where(keep, full, 0.0).astype(BF16)


def own_block(row_ref, index, count):
    width = row_ref.shape[1] // count
    found = row_ref[:, :width]
    for i in range(1, count):
        found = jnp.where(index == i, row_ref[:, i * width : (i + 1) * width], found)
    return found


def part_units(units):
    sizes = [1]
    while sum(sizes) < units:
        left = units - sum(sizes)
        sizes.append(min(2, left) if len(sizes) < 3 else left)
    return tuple(sizes)


def early_modes(block):
    return 1


def partner(place, d, size):
    return lax.rem(place + d, size)


def far_first(size):
    return sorted(range(1, size), key=lambda d: abs(d - size // 2))


def kernel(
    n_row, n_col, parts, outs,
    temp_hbm, hum_hbm, absorb, solar, emission, sunlit, project, restore,
    east_hbm, north_hbm, east_weight, north_weight, east_eigen, north_eigen, coupling,
    out,
    temp, hum, forcing, east, north, east_t, spread_p, spread_r, roots,
    modal, lines, moved, turned, back, joined, solved, gathered,
    in_sem, basis_sem, own_sem,
    z1_send, z1_recv, y1_send, y1_recv, y2_send, y2_recv, z2_send, z2_recv,
):
    levels, east_local, north_local = temp.shape
    modes = project.shape[0]
    bands = absorb.shape[0]
    block = modes // n_col
    nx = east.shape[0]
    ny = north.shape[0]
    east_part = nx // n_row
    starts = [sum(parts[:p]) for p in range(len(parts))]
    r = lax.axis_index("row")
    c = lax.axis_index("col")

    barrier = pltpu.get_barrier_semaphore()
    for d in range(1, n_col):
        pl.semaphore_signal(
            barrier, inc=1, device_id=(r, lax.rem(c + d, n_col)), device_id_type=MESH
        )
    for d in range(1, n_row):
        pl.semaphore_signal(
            barrier, inc=1, device_id=(lax.rem(r + d, n_row), c), device_id_type=MESH
        )

    def fetch(part):
        rows = pl.ds(starts[part] * PAIR, parts[part] * PAIR)
        return (
            pltpu.make_async_copy(
                temp_hbm.at[:, rows, :], temp.at[:, rows, :], in_sem.at[0, part]
            ),
            pltpu.make_async_copy(
                hum_hbm.at[:, rows, :], hum.at[:, rows, :], in_sem.at[1, part]
            ),
        )

    fetches = [fetch(part) for part in range(len(parts))]
    for pair in fetches:
        for copy in pair:
            copy.start()
    get_east = pltpu.make_async_copy(east_hbm, east, basis_sem.at[0])
    get_north = pltpu.make_async_copy(north_hbm, north, basis_sem.at[1])

    spread_p[...] = spread(project[...])

    lit = sunlit[r, c]
    width = min(128, north_local)
    emit = [emission[b] for b in range(bands)]
    emit_all = emit[0]
    for b in range(1, bands):
        emit_all = emit_all + emit[b]
    unroll = 8

    def radiate(a, carry):
        top = pl.multiple_of(a * PAIR, PAIR)
        for lane in range(north_local // width):
            lanes = slice(lane * width, (lane + 1) * width)
            place = (top + lax.broadcasted_iota(jnp.int32, (PAIR, width), 0)) * north_local + (
                lane * width + lax.broadcasted_iota(jnp.int32, (PAIR, width), 1)
            )
            mask = (place < lit).astype(F32)
            beams = tuple(solar[b] * mask for b in range(bands))
            total = beams[0]
            for b in range(1, bands):
                total = total + beams[b]

            def level_group(group, state):
                beams, total = state
                for step in range(unroll):
                    level = group * unroll + step
                    t = temp[level, pl.ds(top, PAIR), lanes].astype(F32)
                    h = hum[level, pl.ds(top, PAIR), lanes].astype(F32)
                    new_beams = []
                    lower = None
                    glow = None
                    for b in range(bands):
                        passed = jnp.exp2(h * (absorb[b, level] * (-math.log2(math.e))))
                        beam = beams[b] * passed
                        new_beams.append(beam)
                        lower = beam if lower is None else lower + beam
                        part = passed * emit[b]
                        glow = part if glow is None else glow + part
                    value = (t + (total - lower)) - (emit_all - glow) * t
                    beams, total = tuple(new_beams), lower
                    at = pl.ds(pl.multiple_of(level * SUB, SUB), SUB)
                    forcing[2 * a, at, lanes] = value[:SUB]
                    forcing[2 * a + 1, at, lanes] = value[SUB:]
                return beams, total

            lax.fori_loop(0, levels // unroll, level_group, (beams, total))
        halves = []
        for s in range(2):
            got = jnp.dot(
                spread_p[...], forcing[2 * a + s].astype(BF16), preferred_element_type=F32
            )
            halves.append(got.reshape(modes, SUB, north_local))
        modal[:, pl.ds(top, PAIR), :] = jnp.concatenate(halves, axis=1).astype(BF16)
        return carry

    early = early_modes(block)

    def z1_copy(d, piece, first, count, start, rows):
        to = partner(c, d, n_col)
        return pltpu.make_async_remote_copy(
            src_ref=modal.at[pl.ds(to * block + first, count), pl.ds(start, rows), :],
            dst_ref=lines.at[
                pl.ds(first, count), pl.ds(pl.multiple_of(c * east_local + start, PAIR), rows), :
            ],
            send_sem=z1_send.at[piece, d],
            recv_sem=z1_recv.at[piece, d],
            device_id=(r, to),
            device_id_type=MESH,
        )

    def z1_early(part, d):
        count = block if part == 0 else early
        return z1_copy(d, part, 0, count, starts[part] * PAIR, parts[part] * PAIR)

    late_start = parts[0] * PAIR
    late = range(early, block) if late_start < east_local else ()

    def z1_late(k, d):
        return z1_copy(d, len(parts) + k - early, k, 1, late_start, east_local - late_start)

    def z1_own(k):
        return pltpu.make_async_copy(
            modal.at[c * block + k],
            lines.at[k, pl.ds(pl.multiple_of(c * east_local, PAIR), east_local), :],
            own_sem.at[0, k],
        )

    order_col = far_first(n_col)
    order_row = far_first(n_row)
    for part in range(len(parts)):
        for copy in fetches[part]:
            copy.wait()
        if part == len(parts) - 1:
            get_east.start()
            get_north.start()
        lax.fori_loop(starts[part], starts[part] + parts[part], radiate, 0)
        if part == 0:
            pl.semaphore_wait(barrier, n_col - 1 + n_row - 1)
        for d in order_col:
            z1_early(part, d).start()
    for k in late:
        for d in order_col:
            z1_late(k, d).start()
    for k in range(block):
        z1_own(k).start()

    spread_r[...] = spread(jnp.transpose(restore[...]))
    get_east.wait()

    turn = min(128, nx)

    def transpose_block(q, carry):
        at = pl.multiple_of(q * turn, turn)
        piece = jnp.transpose(east[pl.ds(at, turn), :].astype(F32))
        east_t[:, pl.ds(at, turn)] = (piece * east_weight[:, pl.ds(at, turn)]).astype(BF16)
        return carry

    lax.fori_loop(0, nx // turn, transpose_block, 0)
    roots[...] = jnp.transpose(
        jnp.broadcast_to(own_block(east_eigen, r, n_row), (128, east_part))
    )
    weight = own_block(north_weight, r, n_row)
    get_north.wait()

    def y1_copy(k, d):
        return pltpu.make_async_remote_copy(
            src_ref=moved.at[k, d],
            dst_ref=turned.at[k, r],
            send_sem=y1_send.at[k, d],
            recv_sem=y1_recv.at[k, d],
            device_id=(lax.rem(r + d, n_row), c),
            device_id_type=MESH,
        )

    def y2_copy(k, d):
        return pltpu.make_async_remote_copy(
            src_ref=back.at[k, d],
            dst_ref=joined.at[k, pl.ds(pl.multiple_of(r * east_part, PAIR), east_part), :],
            send_sem=y2_send.at[k, d],
            recv_sem=y2_recv.at[k, d],
            device_id=(lax.rem(r + d, n_row), c),
            device_id_type=MESH,
        )

    def z2_copy(k, piece, pieces, d):
        to = partner(c, d, n_col)
        rows = east_local // pieces
        start = piece * rows
        return pltpu.make_async_remote_copy(
            src_ref=solved.at[
                k, pl.ds(pl.multiple_of(to * east_local + start, PAIR), rows), :
            ],
            dst_ref=gathered.at[c * block + k, pl.ds(start, rows), :],
            send_sem=z2_send.at[k, piece, d],
            recv_sem=z2_recv.at[k, piece, d],
            device_id=(r, to),
            device_id_type=MESH,
        )

    def z2_own(k):
        return pltpu.make_async_copy(
            solved.at[k, pl.ds(pl.multiple_of(c * east_local, PAIR), east_local), :],
            gathered.at[c * block + k],
            own_sem.at[1, k],
        )

    def x_forward(k):
        z1_own(k).wait()

        @pl.when(k == 0)
        def _():
            for part in range(len(parts)):
                for d in order_col:
                    z1_early(part, d).wait_recv()

        if late:

            @pl.when(k >= early)
            def _():
                for d in order_col:
                    z1_late(k, d).wait_recv()

        for d in order_row + [0]:
            to = lax.rem(r + d, n_row)
            got = jnp.dot(
                east_t[pl.ds(pl.multiple_of(to * east_part, PAIR), east_part), :],
                lines[k],
                preferred_element_type=F32,
            )
            got = (got * weight).astype(BF16)
            if d == 0:
                turned[k, r] = got
            else:
                moved[k, d] = got
                y1_copy(k, d).start()

    def y_both(k):
        for d in order_row:
            y1_copy(k, d).wait_recv()
        total = None
        for source in range(n_row):
            term = jnp.dot(
                turned[k, source],
                north[source * north_local : (source + 1) * north_local, :],
                preferred_element_type=F32,
            )
            total = term if total is None else total + term
        side = roots[...]
        gravity = coupling[c * block + k]
        pieces = []
        for lane in range(ny // 128):
            lanes = slice(lane * 128, (lane + 1) * 128)
            divisor = 1.0 + gravity * (side + north_eigen[:, lanes])
            pieces.append((total[:, lanes] / divisor).astype(BF16))
        scaled = jnp.concatenate(pieces, axis=1)
        for d in order_row + [0]:
            to = lax.rem(r + d, n_row)
            got = lax.dot_general(
                scaled,
                north[pl.ds(pl.multiple_of(to * north_local, PAIR), north_local), :],
                (((1,), (1,)), ((), ())),
                preferred_element_type=F32,
            ).astype(BF16)
            if d == 0:
                joined[k, pl.ds(pl.multiple_of(r * east_part, PAIR), east_part), :] = got
            else:
                back[k, d] = got
                y2_copy(k, d).start()

    def x_back(k):
        for d in order_row:
            y2_copy(k, d).wait_recv()
        rows = min(256, nx)
        for q in range(nx // rows):
            solved[k, q * rows : (q + 1) * rows, :] = jnp.dot(
                east[q * rows : (q + 1) * rows, :], joined[k], preferred_element_type=F32
            ).astype(BF16)

        @pl.when(k < block - 1)
        def _():
            for d in order_col:
                z2_copy(k, 0, 1, d).start()

        @pl.when(k == block - 1)
        def _():
            for piece in range(outs):
                for d in order_col:
                    z2_copy(k, piece, outs, d).start()

        z2_own(k).start()

    def stage(t, carry):
        @pl.when(t >= 2)
        def _():
            x_back(t - 2)

        @pl.when(t < block)
        def _():
            x_forward(t)

        @pl.when(jnp.logical_and(t >= 1, t < block + 1))
        def _():
            y_both(t - 1)

        return carry

    lax.fori_loop(0, block + 2, stage, 0)

    for k in range(block):
        z2_own(k).wait()

    def finish(a, carry):
        top = pl.multiple_of(a * PAIR, PAIR)
        rows = pl.ds(top, PAIR)
        change = gathered[:, rows, :].astype(F32) - modal[:, rows, :].astype(F32)
        halves = []
        for s in range(2):
            part = change[:, s * SUB : (s + 1) * SUB, :].reshape(modes * SUB, north_local)
            got = forcing[2 * a + s] + jnp.dot(
                spread_r[...], part.astype(BF16), preferred_element_type=F32
            )
            halves.append(got.reshape(levels, SUB, north_local))
        out[:, rows, :] = jnp.concatenate(halves, axis=1).astype(BF16)
        return carry

    out_rows = east_local // outs
    per_out = out_rows // PAIR

    for part in range(outs):
        if part == 0:
            for k in range(block - 1):
                for d in order_col:
                    z2_copy(k, 0, 1, d).wait_recv()
        for d in order_col:
            z2_copy(block - 1, part, outs, d).wait_recv()
        lax.fori_loop(part * per_out, (part + 1) * per_out, finish, 0)

    for d in order_col:
        for part in range(len(parts)):
            z1_early(part, d).wait_send()
        for k in late:
            z1_late(k, d).wait_send()
        for k in range(block - 1):
            z2_copy(k, 0, 1, d).wait_send()
        for part in range(outs):
            z2_copy(block - 1, part, outs, d).wait_send()
    for k in range(block):
        for d in order_row:
            y1_copy(k, d).wait_send()
            y2_copy(k, d).wait_send()


def local(
    n_row, n_col,
    potential_temp, humidity, absorb, solar_flux, emission, sunlit, project, restore,
    east_basis, north_basis, east_weight, north_weight, east_eigen, north_eigen, coupling,
):
    levels, east_local, north_local = potential_temp.shape
    modes = project.shape[0]
    nx, ny = east_basis.shape[0], north_basis.shape[0]
    block = modes // n_col
    east_part = nx // n_row
    parts = part_units(east_local // PAIR)
    pieces = len(parts) + block - early_modes(block)
    outs = min(4, east_local // PAIR)
    hbm = pl.BlockSpec(memory_space=pl.ANY)
    smem = pl.BlockSpec(memory_space=pltpu.SMEM)
    vmem = pl.BlockSpec(memory_space=pltpu.VMEM)
    dma = pltpu.SemaphoreType.DMA
    grid_lines = (block, nx, north_local)
    return pl.pallas_call(
        functools.partial(kernel, n_row, n_col, parts, outs),
        out_shape=pltpu.VMEM(potential_temp.shape, BF16),
        in_specs=[
            hbm, hbm, smem, smem, smem, smem, vmem, vmem,
            hbm, hbm, vmem, vmem, vmem, vmem, smem,
        ],
        out_specs=vmem,
        scratch_shapes=[
            pltpu.VMEM(potential_temp.shape, BF16),
            pltpu.VMEM(humidity.shape, BF16),
            pltpu.VMEM((east_local // SUB, levels * SUB, north_local), F32),
            pltpu.VMEM((nx, nx), BF16),
            pltpu.VMEM((ny, ny), BF16),
            pltpu.VMEM((nx, nx), BF16),
            pltpu.VMEM((modes * SUB, levels * SUB), BF16),
            pltpu.VMEM((levels * SUB, modes * SUB), BF16),
            pltpu.VMEM((east_part, 128), F32),
            pltpu.VMEM((modes, east_local, north_local), BF16),
            pltpu.VMEM(grid_lines, BF16),
            pltpu.VMEM((block, n_row, east_part, north_local), BF16),
            pltpu.VMEM((block, n_row, east_part, north_local), BF16),
            pltpu.VMEM((block, n_row, east_part, north_local), BF16),
            pltpu.VMEM(grid_lines, BF16),
            pltpu.VMEM(grid_lines, BF16),
            pltpu.VMEM((modes, east_local, north_local), BF16),
            dma((2, len(parts))),
            dma((2,)),
            dma((2, block)),
            dma((pieces, n_col)),
            dma((pieces, n_col)),
            dma((block, n_row)),
            dma((block, n_row)),
            dma((block, n_row)),
            dma((block, n_row)),
            dma((block, outs, n_col)),
            dma((block, outs, n_col)),
        ],
        compiler_params=pltpu.CompilerParams(
            collective_id=0, has_side_effects=True, vmem_limit_bytes=54 * 1024 * 1024
        ),
        name="semi_implicit_step",
    )(
        potential_temp, humidity, absorb, solar_flux, emission, sunlit, project, restore.T,
        east_basis, north_basis,
        east_weight.reshape(1, nx),
        north_weight.reshape(1, ny),
        east_eigen.reshape(1, nx),
        north_eigen.reshape(1, ny),
        coupling,
    )


def solution(mesh):
    split = P(None, "col", "row")
    return jax.shard_map(
        functools.partial(local, mesh.shape["row"], mesh.shape["col"]),
        mesh=mesh,
        in_specs=(split, split) + (P(),) * 13,
        out_specs=split,
        check_vma=False,
    )
```

```python
import functools
import math

import jax
import jax.numpy as jnp
from jax import lax
from jax.experimental import pallas as pl
from jax.experimental.pallas import tpu as pltpu
from jax.sharding import PartitionSpec as P

SUB = 8
PAIR = 16
MESH = pl.DeviceIdType.MESH
F32 = jnp.float32
BF16 = jnp.bfloat16
SIZES = (1, 2, 2, 3)
EARLY = 4
SCHED = (("f", 0), ("y", 1), ("b", 2))


def spread(matrix):
    rows, cols = matrix.shape
    tall = (
        lax.broadcasted_iota(jnp.int32, (rows * SUB, rows), 0) // SUB
        == lax.broadcasted_iota(jnp.int32, (rows * SUB, rows), 1)
    ).astype(F32).astype(BF16)
    wide = (
        lax.broadcasted_iota(jnp.int32, (cols, cols * SUB), 1) // SUB
        == lax.broadcasted_iota(jnp.int32, (cols, cols * SUB), 0)
    ).astype(F32).astype(BF16)
    half = jnp.dot(tall, matrix.astype(BF16), preferred_element_type=F32).astype(BF16)
    full = jnp.dot(half, wide, preferred_element_type=F32)
    shape = (rows * SUB, cols * SUB)
    keep = (
        lax.broadcasted_iota(jnp.int32, shape, 0) % SUB
        == lax.broadcasted_iota(jnp.int32, shape, 1) % SUB
    )
    return jnp.where(keep, full, 0.0).astype(BF16)


def own_block(row_ref, index, count):
    width = row_ref.shape[1] // count
    found = row_ref[:, :width]
    for i in range(1, count):
        found = jnp.where(index == i, row_ref[:, i * width : (i + 1) * width], found)
    return found


def part_units(units):
    sizes = []
    for size in SIZES:
        if sum(sizes) < units:
            sizes.append(min(size, units - sum(sizes)))
    sizes += [1] * (units - sum(sizes))
    return tuple(sizes)


def early_modes(part, block):
    return min(block, EARLY if part == 0 else 1)


def partner(place, d, size):
    return lax.rem(place + d, size)


def far_first(size):
    return sorted(range(1, size), key=lambda d: abs(d - size // 2))


def kernel(
    n_row, n_col, parts, outs,
    temp_hbm, hum_hbm, absorb, solar, emission, sunlit, project, restore,
    east_hbm, north_hbm, east_weight, north_weight, east_eigen, north_eigen, coupling,
    out,
    temp, hum, forcing, east, north, east_t, spread_p, spread_r, roots,
    modal, lines, moved, turned, back, joined, solved, gathered,
    in_sem, basis_sem,
    z1_send, z1_recv, y1_send, y1_recv, y2_send, y2_recv, z2_send, z2_recv,
):
    levels, east_local, north_local = temp.shape
    modes = project.shape[0]
    bands = absorb.shape[0]
    block = modes // n_col
    nx = east.shape[0]
    ny = north.shape[0]
    east_part = nx // n_row
    starts = [sum(parts[:p]) for p in range(len(parts))]
    r = lax.axis_index("row")
    c = lax.axis_index("col")

    barrier = pltpu.get_barrier_semaphore()
    for d in range(1, n_col):
        pl.semaphore_signal(
            barrier, inc=1, device_id=(r, lax.rem(c + d, n_col)), device_id_type=MESH
        )
    for d in range(1, n_row):
        pl.semaphore_signal(
            barrier, inc=1, device_id=(lax.rem(r + d, n_row), c), device_id_type=MESH
        )

    def drain(ref, sem):
        pltpu.make_async_copy(ref, ref, sem).wait()

    def fetch(part):
        rows = pl.ds(starts[part] * PAIR, parts[part] * PAIR)
        return (
            pltpu.make_async_copy(
                temp_hbm.at[:, rows, :], temp.at[:, rows, :], in_sem.at[0, part]
            ),
            pltpu.make_async_copy(
                hum_hbm.at[:, rows, :], hum.at[:, rows, :], in_sem.at[1, part]
            ),
        )

    fetches = [fetch(part) for part in range(len(parts))]
    for pair in fetches:
        for copy in pair:
            copy.start()
    get_east = pltpu.make_async_copy(east_hbm, east, basis_sem.at[0])
    get_north = pltpu.make_async_copy(north_hbm, north, basis_sem.at[1])

    spread_p[...] = spread(project[...])

    lit = sunlit[r, c]
    width = min(128, north_local)
    emit = [emission[b] for b in range(bands)]
    emit_all = emit[0]
    for b in range(1, bands):
        emit_all = emit_all + emit[b]
    unroll = 8

    def radiate(a, carry):
        top = pl.multiple_of(a * PAIR, PAIR)
        for lane in range(north_local // width):
            lanes = slice(lane * width, (lane + 1) * width)
            place = (top + lax.broadcasted_iota(jnp.int32, (PAIR, width), 0)) * north_local + (
                lane * width + lax.broadcasted_iota(jnp.int32, (PAIR, width), 1)
            )
            mask = (place < lit).astype(F32)
            beams = tuple(solar[b] * mask for b in range(bands))
            total = beams[0]
            for b in range(1, bands):
                total = total + beams[b]

            def level_group(group, state):
                beams, total = state
                for step in range(unroll):
                    level = group * unroll + step
                    t = temp[level, pl.ds(top, PAIR), lanes].astype(F32)
                    h = hum[level, pl.ds(top, PAIR), lanes].astype(F32)
                    new_beams = []
                    lower = None
                    glow = None
                    for b in range(bands):
                        passed = jnp.exp2(h * (absorb[b, level] * (-math.log2(math.e))))
                        beam = beams[b] * passed
                        new_beams.append(beam)
                        lower = beam if lower is None else lower + beam
                        part = passed * emit[b]
                        glow = part if glow is None else glow + part
                    value = (t + (total - lower)) - (emit_all - glow) * t
                    beams, total = tuple(new_beams), lower
                    at = pl.ds(pl.multiple_of(level * SUB, SUB), SUB)
                    forcing[2 * a, at, lanes] = value[:SUB]
                    forcing[2 * a + 1, at, lanes] = value[SUB:]
                return beams, total

            lax.fori_loop(0, levels // unroll, level_group, (beams, total))
        halves = []
        for s in range(2):
            got = jnp.dot(
                spread_p[...], forcing[2 * a + s].astype(BF16), preferred_element_type=F32
            )
            halves.append(got.reshape(modes, SUB, north_local))
        modal[:, pl.ds(top, PAIR), :] = jnp.concatenate(halves, axis=1).astype(BF16)
        return carry

    early = [early_modes(part, block) for part in range(len(parts))]
    late = {}
    for k in range(1, block):
        sent = sum(parts[p] for p in range(len(parts)) if early[p] > k) * PAIR
        if sent < east_local:
            late[k] = sent

    def z1_copy(d, group, first, count, start, rows):
        to = partner(c, d, n_col)
        return pltpu.make_async_remote_copy(
            src_ref=modal.at[pl.ds(to * block + first, count), pl.ds(start, rows), :],
            dst_ref=lines.at[
                pl.ds(first, count), pl.ds(pl.multiple_of(c * east_local + start, PAIR), rows), :
            ],
            send_sem=z1_send,
            recv_sem=z1_recv.at[group],
            device_id=(r, to),
            device_id_type=MESH,
        )

    def z1_early(part, d):
        group = block if early[part] > 1 else 0
        return z1_copy(d, group, 0, early[part], starts[part] * PAIR, parts[part] * PAIR)

    def z1_late(k, d):
        return z1_copy(d, k, k, 1, late[k], east_local - late[k])

    def z1_own(k):
        lines[k, pl.ds(pl.multiple_of(c * east_local, PAIR), east_local), :] = modal[c * block + k]

    order_col = far_first(n_col)
    order_row = far_first(n_row)
    for part in range(len(parts)):
        for copy in fetches[part]:
            copy.wait()
        if part == len(parts) - 1:
            get_east.start()
            get_north.start()
        lax.fori_loop(starts[part], starts[part] + parts[part], radiate, 0)
        if part == 0:
            pl.semaphore_wait(barrier, n_col - 1 + n_row - 1)
        for d in order_col:
            z1_early(part, d).start()
    for k in late:
        for d in order_col:
            z1_late(k, d).start()

    spread_r[...] = spread(jnp.transpose(restore[...]))
    get_east.wait()

    turn = min(128, nx)

    def transpose_block(q, carry):
        at = pl.multiple_of(q * turn, turn)
        piece = jnp.transpose(east[pl.ds(at, turn), :].astype(F32))
        east_t[:, pl.ds(at, turn)] = (piece * east_weight[:, pl.ds(at, turn)]).astype(BF16)
        return carry

    lax.fori_loop(0, nx // turn, transpose_block, 0)
    roots[...] = jnp.transpose(
        jnp.broadcast_to(own_block(east_eigen, r, n_row), (128, east_part))
    )
    weight = own_block(north_weight, r, n_row)
    get_north.wait()

    def y1_copy(k, d):
        return pltpu.make_async_remote_copy(
            src_ref=moved.at[k, d],
            dst_ref=turned.at[k, r],
            send_sem=y1_send,
            recv_sem=y1_recv.at[k],
            device_id=(lax.rem(r + d, n_row), c),
            device_id_type=MESH,
        )

    def y2_copy(k, d):
        return pltpu.make_async_remote_copy(
            src_ref=back.at[k, d],
            dst_ref=joined.at[k, pl.ds(pl.multiple_of(r * east_part, PAIR), east_part), :],
            send_sem=y2_send,
            recv_sem=y2_recv.at[k],
            device_id=(lax.rem(r + d, n_row), c),
            device_id_type=MESH,
        )

    def z2_copy(k, piece, pieces, group, d):
        to = partner(c, d, n_col)
        rows = east_local // pieces
        start = piece * rows
        return pltpu.make_async_remote_copy(
            src_ref=solved.at[
                k, pl.ds(pl.multiple_of(to * east_local + start, PAIR), rows), :
            ],
            dst_ref=gathered.at[c * block + k, pl.ds(start, rows), :],
            send_sem=z2_send,
            recv_sem=z2_recv.at[group],
            device_id=(r, to),
            device_id_type=MESH,
        )

    def z2_own(k):
        gathered[c * block + k] = solved[
            k, pl.ds(pl.multiple_of(c * east_local, PAIR), east_local), :
        ]

    def x_forward(k):
        z1_own(k)

        @pl.when(k == 0)
        def _():
            for count in sorted(set(early)):
                rows = sum(parts[p] for p in range(len(parts)) if early[p] == count) * PAIR
                drain(
                    lines.at[pl.ds(0, count), pl.ds(0, (n_col - 1) * rows), :],
                    z1_recv.at[block if count > 1 else 0],
                )

        for later in late:

            @pl.when(k == later)
            def _():
                rows = (n_col - 1) * (east_local - late[later])
                drain(lines.at[later, pl.ds(0, rows), :], z1_recv.at[later])

        for d in order_row + [0]:
            to = lax.rem(r + d, n_row)
            got = jnp.dot(
                east_t[pl.ds(pl.multiple_of(to * east_part, PAIR), east_part), :],
                lines[k],
                preferred_element_type=F32,
            )
            got = (got * weight).astype(BF16)
            if d == 0:
                turned[k, r] = got
            else:
                moved[k, d] = got
                y1_copy(k, d).start()

    def y_both(k):
        drain(turned.at[k, pl.ds(0, n_row - 1)], y1_recv.at[k])
        total = None
        for source in range(n_row):
            term = jnp.dot(
                turned[k, source],
                north[source * north_local : (source + 1) * north_local, :],
                preferred_element_type=F32,
            )
            total = term if total is None else total + term
        side = roots[...]
        gravity = coupling[c * block + k]
        pieces = []
        for lane in range(ny // 128):
            lanes = slice(lane * 128, (lane + 1) * 128)
            divisor = 1.0 + gravity * (side + north_eigen[:, lanes])
            pieces.append((total[:, lanes] / divisor).astype(BF16))
        scaled = jnp.concatenate(pieces, axis=1)
        for d in order_row + [0]:
            to = lax.rem(r + d, n_row)
            got = lax.dot_general(
                scaled,
                north[pl.ds(pl.multiple_of(to * north_local, PAIR), north_local), :],
                (((1,), (1,)), ((), ())),
                preferred_element_type=F32,
            ).astype(BF16)
            if d == 0:
                joined[k, pl.ds(pl.multiple_of(r * east_part, PAIR), east_part), :] = got
            else:
                back[k, d] = got
                y2_copy(k, d).start()

    def x_back(k):
        drain(joined.at[k, pl.ds(0, (n_row - 1) * east_part), :], y2_recv.at[k])
        rows = min(256, nx)
        for q in range(nx // rows):
            solved[k, q * rows : (q + 1) * rows, :] = jnp.dot(
                east[q * rows : (q + 1) * rows, :], joined[k], preferred_element_type=F32
            ).astype(BF16)

        @pl.when(k < block - 1)
        def _():
            for d in order_col:
                z2_copy(k, 0, 1, outs, d).start()

        @pl.when(k == block - 1)
        def _():
            for piece in range(outs):
                for d in order_col:
                    z2_copy(k, piece, outs, piece, d).start()

        z2_own(k)

    run = {"f": x_forward, "y": y_both, "b": x_back}

    def stage(t, carry):
        for name, lag in SCHED:

            @pl.when(jnp.logical_and(t >= lag, t < block + lag))
            def _():
                run[name](t - lag)

        return carry

    lax.fori_loop(0, block + max(lag for _, lag in SCHED), stage, 0)

    def finish(a, carry):
        top = pl.multiple_of(a * PAIR, PAIR)
        rows = pl.ds(top, PAIR)
        change = gathered[:, rows, :].astype(F32) - modal[:, rows, :].astype(F32)
        halves = []
        for s in range(2):
            part = change[:, s * SUB : (s + 1) * SUB, :].reshape(modes * SUB, north_local)
            got = forcing[2 * a + s] + jnp.dot(
                spread_r[...], part.astype(BF16), preferred_element_type=F32
            )
            halves.append(got.reshape(levels, SUB, north_local))
        out[:, rows, :] = jnp.concatenate(halves, axis=1).astype(BF16)
        return carry

    out_rows = east_local // outs
    per_out = out_rows // PAIR

    for part in range(outs):
        if part == 0 and block > 1:
            drain(gathered.at[pl.ds(0, (block - 1) * (n_col - 1))], z2_recv.at[outs])
        drain(
            gathered.at[pl.ds(0, n_col - 1), pl.ds(0, out_rows), :], z2_recv.at[part]
        )
        lax.fori_loop(part * per_out, (part + 1) * per_out, finish, 0)

    drain(modal.at[pl.ds(0, block * (n_col - 1))], z1_send)
    drain(moved.at[:, pl.ds(0, n_row - 1)], y1_send)
    drain(back.at[:, pl.ds(0, n_row - 1)], y2_send)
    drain(solved.at[:, pl.ds(0, (n_col - 1) * east_local), :], z2_send)


def local(
    n_row, n_col,
    potential_temp, humidity, absorb, solar_flux, emission, sunlit, project, restore,
    east_basis, north_basis, east_weight, north_weight, east_eigen, north_eigen, coupling,
):
    levels, east_local, north_local = potential_temp.shape
    modes = project.shape[0]
    nx, ny = east_basis.shape[0], north_basis.shape[0]
    block = modes // n_col
    east_part = nx // n_row
    parts = part_units(east_local // PAIR)
    outs = min(4, east_local // PAIR)
    hbm = pl.BlockSpec(memory_space=pl.ANY)
    smem = pl.BlockSpec(memory_space=pltpu.SMEM)
    vmem = pl.BlockSpec(memory_space=pltpu.VMEM)
    dma = pltpu.SemaphoreType.DMA
    grid_lines = (block, nx, north_local)
    return pl.pallas_call(
        functools.partial(kernel, n_row, n_col, parts, outs),
        out_shape=pltpu.VMEM(potential_temp.shape, BF16),
        in_specs=[
            hbm, hbm, smem, smem, smem, smem, vmem, vmem,
            hbm, hbm, vmem, vmem, vmem, vmem, smem,
        ],
        out_specs=vmem,
        scratch_shapes=[
            pltpu.VMEM(potential_temp.shape, BF16),
            pltpu.VMEM(humidity.shape, BF16),
            pltpu.VMEM((east_local // SUB, levels * SUB, north_local), F32),
            pltpu.VMEM((nx, nx), BF16),
            pltpu.VMEM((ny, ny), BF16),
            pltpu.VMEM((nx, nx), BF16),
            pltpu.VMEM((modes * SUB, levels * SUB), BF16),
            pltpu.VMEM((levels * SUB, modes * SUB), BF16),
            pltpu.VMEM((east_part, 128), F32),
            pltpu.VMEM((modes, east_local, north_local), BF16),
            pltpu.VMEM(grid_lines, BF16),
            pltpu.VMEM((block, n_row, east_part, north_local), BF16),
            pltpu.VMEM((block, n_row, east_part, north_local), BF16),
            pltpu.VMEM((block, n_row, east_part, north_local), BF16),
            pltpu.VMEM(grid_lines, BF16),
            pltpu.VMEM(grid_lines, BF16),
            pltpu.VMEM((modes, east_local, north_local), BF16),
            dma((2, len(parts))),
            dma((2,)),
            dma(()),
            dma((block + 1,)),
            dma(()),
            dma((block,)),
            dma(()),
            dma((block,)),
            dma(()),
            dma((outs + 1,)),
        ],
        compiler_params=pltpu.CompilerParams(
            collective_id=0, has_side_effects=True, vmem_limit_bytes=54 * 1024 * 1024
        ),
        name="semi_implicit_step",
    )(
        potential_temp, humidity, absorb, solar_flux, emission, sunlit, project, restore.T,
        east_basis, north_basis,
        east_weight.reshape(1, nx),
        north_weight.reshape(1, ny),
        east_eigen.reshape(1, nx),
        north_eigen.reshape(1, ny),
        coupling,
    )


def solution(mesh):
    split = P(None, "col", "row")
    return jax.shard_map(
        functools.partial(local, mesh.shape["row"], mesh.shape["col"]),
        mesh=mesh,
        in_specs=(split, split) + (P(),) * 13,
        out_specs=split,
        check_vma=False,
    )
```

```python
import functools
import math

import jax
import jax.numpy as jnp
from jax import lax
from jax.experimental import pallas as pl
from jax.experimental.pallas import tpu as pltpu
from jax.sharding import PartitionSpec as P

SUB = 8
PAIR = 16
MESH = pl.DeviceIdType.MESH
F32 = jnp.float32
BF16 = jnp.bfloat16
SIZES = (1, 2, 2, 3)
EARLY = 4
SCHED = (("y", 1), ("f", 0), ("b", 1))


def spread(matrix):
    rows, cols = matrix.shape
    tall = (
        lax.broadcasted_iota(jnp.int32, (rows * SUB, rows), 0) // SUB
        == lax.broadcasted_iota(jnp.int32, (rows * SUB, rows), 1)
    ).astype(F32).astype(BF16)
    wide = (
        lax.broadcasted_iota(jnp.int32, (cols, cols * SUB), 1) // SUB
        == lax.broadcasted_iota(jnp.int32, (cols, cols * SUB), 0)
    ).astype(F32).astype(BF16)
    half = jnp.dot(tall, matrix.astype(BF16), preferred_element_type=F32).astype(BF16)
    full = jnp.dot(half, wide, preferred_element_type=F32)
    shape = (rows * SUB, cols * SUB)
    keep = (
        lax.broadcasted_iota(jnp.int32, shape, 0) % SUB
        == lax.broadcasted_iota(jnp.int32, shape, 1) % SUB
    )
    return jnp.where(keep, full, 0.0).astype(BF16)


def own_block(row_ref, index, count):
    width = row_ref.shape[1] // count
    found = row_ref[:, :width]
    for i in range(1, count):
        found = jnp.where(index == i, row_ref[:, i * width : (i + 1) * width], found)
    return found


def part_units(units):
    sizes = []
    for size in SIZES:
        if sum(sizes) < units:
            sizes.append(min(size, units - sum(sizes)))
    sizes += [1] * (units - sum(sizes))
    return tuple(sizes)


def early_modes(part, block):
    return min(block, EARLY if part == 0 else 1)


def partner(place, d, size):
    return lax.rem(place + d, size)


def far_first(size):
    return sorted(range(1, size), key=lambda d: abs(d - size // 2))


def kernel(
    n_row, n_col, parts,
    temp_hbm, hum_hbm, absorb, solar, emission, sunlit, project, restore,
    east_hbm, north_hbm, east_weight, north_weight, east_eigen, north_eigen, coupling,
    forcing, gathered, spread_r,
    temp, hum, east, north, east_t, spread_p, roots,
    modal, lines, moved, turned, back, joined, solved,
    in_sem, basis_sem,
    z1_send, z1_recv, y1_send, y1_recv, y2_send, y2_recv, z2_send, z2_recv,
):
    levels, east_local, north_local = temp.shape
    modes = project.shape[0]
    bands = absorb.shape[0]
    block = modes // n_col
    nx = east.shape[0]
    ny = north.shape[0]
    east_part = nx // n_row
    starts = [sum(parts[:p]) for p in range(len(parts))]
    r = lax.axis_index("row")
    c = lax.axis_index("col")

    barrier = pltpu.get_barrier_semaphore()
    for d in range(1, n_col):
        pl.semaphore_signal(
            barrier, inc=1, device_id=(r, lax.rem(c + d, n_col)), device_id_type=MESH
        )
    for d in range(1, n_row):
        pl.semaphore_signal(
            barrier, inc=1, device_id=(lax.rem(r + d, n_row), c), device_id_type=MESH
        )

    def drain(ref, sem):
        pltpu.make_async_copy(ref, ref, sem).wait()

    def fetch(part):
        rows = pl.ds(starts[part] * PAIR, parts[part] * PAIR)
        return (
            pltpu.make_async_copy(
                temp_hbm.at[:, rows, :], temp.at[:, rows, :], in_sem.at[0, part]
            ),
            pltpu.make_async_copy(
                hum_hbm.at[:, rows, :], hum.at[:, rows, :], in_sem.at[1, part]
            ),
        )

    fetches = [fetch(part) for part in range(len(parts))]
    for pair in fetches:
        for copy in pair:
            copy.start()
    get_east = pltpu.make_async_copy(east_hbm, east, basis_sem.at[0])
    get_north = pltpu.make_async_copy(north_hbm, north, basis_sem.at[1])

    spread_p[...] = spread(project[...])

    lit = sunlit[r, c]
    width = min(128, north_local)
    emit = [emission[b] for b in range(bands)]
    emit_all = emit[0]
    for b in range(1, bands):
        emit_all = emit_all + emit[b]
    unroll = 8

    def radiate(a, carry):
        top = pl.multiple_of(a * PAIR, PAIR)
        for lane in range(north_local // width):
            lanes = slice(lane * width, (lane + 1) * width)
            place = (top + lax.broadcasted_iota(jnp.int32, (PAIR, width), 0)) * north_local + (
                lane * width + lax.broadcasted_iota(jnp.int32, (PAIR, width), 1)
            )
            mask = (place < lit).astype(F32)
            beams = tuple(solar[b] * mask for b in range(bands))
            total = beams[0]
            for b in range(1, bands):
                total = total + beams[b]

            def level_group(group, state):
                beams, total = state
                for step in range(unroll):
                    level = group * unroll + step
                    t = temp[level, pl.ds(top, PAIR), lanes].astype(F32)
                    h = hum[level, pl.ds(top, PAIR), lanes].astype(F32)
                    new_beams = []
                    lower = None
                    glow = None
                    for b in range(bands):
                        passed = jnp.exp2(h * (absorb[b, level] * (-math.log2(math.e))))
                        beam = beams[b] * passed
                        new_beams.append(beam)
                        lower = beam if lower is None else lower + beam
                        part = passed * emit[b]
                        glow = part if glow is None else glow + part
                    value = (t + (total - lower)) - (emit_all - glow) * t
                    beams, total = tuple(new_beams), lower
                    at = pl.ds(pl.multiple_of(level * SUB, SUB), SUB)
                    forcing[2 * a, at, lanes] = value[:SUB]
                    forcing[2 * a + 1, at, lanes] = value[SUB:]
                return beams, total

            lax.fori_loop(0, levels // unroll, level_group, (beams, total))
        halves = []
        for s in range(2):
            got = jnp.dot(
                spread_p[...], forcing[2 * a + s].astype(BF16), preferred_element_type=F32
            )
            halves.append(got.reshape(modes, SUB, north_local))
        modal[:, pl.ds(top, PAIR), :] = jnp.concatenate(halves, axis=1).astype(BF16)
        return carry

    early = [early_modes(part, block) for part in range(len(parts))]
    late = {}
    for k in range(1, block):
        sent = sum(parts[p] for p in range(len(parts)) if early[p] > k) * PAIR
        if sent < east_local:
            late[k] = sent

    def z1_copy(d, group, first, count, start, rows):
        to = partner(c, d, n_col)
        return pltpu.make_async_remote_copy(
            src_ref=modal.at[pl.ds(to * block + first, count), pl.ds(start, rows), :],
            dst_ref=lines.at[
                pl.ds(first, count), pl.ds(pl.multiple_of(c * east_local + start, PAIR), rows), :
            ],
            send_sem=z1_send,
            recv_sem=z1_recv.at[group],
            device_id=(r, to),
            device_id_type=MESH,
        )

    def z1_early(part, d):
        group = block if early[part] > 1 else 0
        return z1_copy(d, group, 0, early[part], starts[part] * PAIR, parts[part] * PAIR)

    def z1_late(k, d):
        return z1_copy(d, k, k, 1, late[k], east_local - late[k])

    def z1_own(k):
        lines[k, pl.ds(pl.multiple_of(c * east_local, PAIR), east_local), :] = modal[c * block + k]

    order_col = far_first(n_col)
    order_row = far_first(n_row)
    for part in range(len(parts)):
        for copy in fetches[part]:
            copy.wait()
        if part == len(parts) - 1:
            get_east.start()
            get_north.start()
        lax.fori_loop(starts[part], starts[part] + parts[part], radiate, 0)
        if part == 0:
            pl.semaphore_wait(barrier, n_col - 1 + n_row - 1)
        for d in order_col:
            z1_early(part, d).start()
    for k in late:
        for d in order_col:
            z1_late(k, d).start()

    spread_r[...] = spread(jnp.transpose(restore[...]))

    def take_modal(a, carry):
        rows = pl.ds(pl.multiple_of(a * PAIR, PAIR), PAIR)
        field = modal[:, rows, :].astype(F32)
        for s in range(2):
            part = field[:, s * SUB : (s + 1) * SUB, :].reshape(modes * SUB, north_local)
            forcing[2 * a + s] -= jnp.dot(
                spread_r[...], part.astype(BF16), preferred_element_type=F32
            )
        return carry

    lax.fori_loop(0, east_local // PAIR, take_modal, 0)
    get_east.wait()

    turn = min(128, nx)

    def transpose_block(q, carry):
        at = pl.multiple_of(q * turn, turn)
        piece = jnp.transpose(east[pl.ds(at, turn), :].astype(F32))
        east_t[:, pl.ds(at, turn)] = (piece * east_weight[:, pl.ds(at, turn)]).astype(BF16)
        return carry

    lax.fori_loop(0, nx // turn, transpose_block, 0)
    roots[...] = jnp.transpose(
        jnp.broadcast_to(own_block(east_eigen, r, n_row), (128, east_part))
    )
    weight = own_block(north_weight, r, n_row)
    get_north.wait()

    def y1_copy(k, d):
        return pltpu.make_async_remote_copy(
            src_ref=moved.at[k, d],
            dst_ref=turned.at[k, r],
            send_sem=y1_send,
            recv_sem=y1_recv.at[k],
            device_id=(lax.rem(r + d, n_row), c),
            device_id_type=MESH,
        )

    def y2_copy(k, d):
        return pltpu.make_async_remote_copy(
            src_ref=back.at[k, d],
            dst_ref=joined.at[k, pl.ds(pl.multiple_of(r * east_part, PAIR), east_part), :],
            send_sem=y2_send,
            recv_sem=y2_recv.at[k],
            device_id=(lax.rem(r + d, n_row), c),
            device_id_type=MESH,
        )

    def z2_copy(k, d):
        to = partner(c, d, n_col)
        return pltpu.make_async_remote_copy(
            src_ref=solved.at[k, pl.ds(pl.multiple_of(to * east_local, PAIR), east_local), :],
            dst_ref=gathered.at[c * block + k],
            send_sem=z2_send,
            recv_sem=z2_recv,
            device_id=(r, to),
            device_id_type=MESH,
        )

    def z2_own(k):
        gathered[c * block + k] = solved[
            k, pl.ds(pl.multiple_of(c * east_local, PAIR), east_local), :
        ]

    def x_forward(k):
        z1_own(k)

        @pl.when(k == 0)
        def _():
            for count in sorted(set(early)):
                rows = sum(parts[p] for p in range(len(parts)) if early[p] == count) * PAIR
                drain(
                    lines.at[pl.ds(0, count), pl.ds(0, (n_col - 1) * rows), :],
                    z1_recv.at[block if count > 1 else 0],
                )

        for later in late:

            @pl.when(k == later)
            def _():
                rows = (n_col - 1) * (east_local - late[later])
                drain(lines.at[later, pl.ds(0, rows), :], z1_recv.at[later])

        for d in order_row + [0]:
            to = lax.rem(r + d, n_row)
            got = jnp.dot(
                east_t[pl.ds(pl.multiple_of(to * east_part, PAIR), east_part), :],
                lines[k],
                preferred_element_type=F32,
            )
            got = (got * weight).astype(BF16)
            if d == 0:
                turned[k, r] = got
            else:
                moved[k, d] = got
                y1_copy(k, d).start()

    def y_both(k):
        drain(turned.at[k, pl.ds(0, n_row - 1)], y1_recv.at[k])
        total = None
        for source in range(n_row):
            term = jnp.dot(
                turned[k, source],
                north[source * north_local : (source + 1) * north_local, :],
                preferred_element_type=F32,
            )
            total = term if total is None else total + term
        side = roots[...]
        gravity = coupling[c * block + k]
        pieces = []
        for lane in range(ny // 128):
            lanes = slice(lane * 128, (lane + 1) * 128)
            divisor = 1.0 + gravity * (side + north_eigen[:, lanes])
            pieces.append((total[:, lanes] / divisor).astype(BF16))
        scaled = jnp.concatenate(pieces, axis=1)
        for d in order_row + [0]:
            to = lax.rem(r + d, n_row)
            got = lax.dot_general(
                scaled,
                north[pl.ds(pl.multiple_of(to * north_local, PAIR), north_local), :],
                (((1,), (1,)), ((), ())),
                preferred_element_type=F32,
            ).astype(BF16)
            if d == 0:
                joined[k, pl.ds(pl.multiple_of(r * east_part, PAIR), east_part), :] = got
            else:
                back[k, d] = got
                y2_copy(k, d).start()

    def x_back(k):
        drain(joined.at[k, pl.ds(0, (n_row - 1) * east_part), :], y2_recv.at[k])
        rows = min(256, nx)
        for q in range(nx // rows):
            solved[k, q * rows : (q + 1) * rows, :] = jnp.dot(
                east[q * rows : (q + 1) * rows, :], joined[k], preferred_element_type=F32
            ).astype(BF16)

        for d in order_col:
            z2_copy(k, d).start()
        z2_own(k)

    run = {"f": x_forward, "y": y_both, "b": x_back}

    def stage(t, carry):
        for name, lag in SCHED:

            @pl.when(jnp.logical_and(t >= lag, t < block + lag))
            def _():
                run[name](t - lag)

        return carry

    lax.fori_loop(0, block + max(lag for _, lag in SCHED), stage, 0)

    drain(gathered.at[pl.ds(0, block * (n_col - 1))], z2_recv)
    drain(modal.at[pl.ds(0, block * (n_col - 1))], z1_send)
    drain(moved.at[:, pl.ds(0, n_row - 1)], y1_send)
    drain(back.at[:, pl.ds(0, n_row - 1)], y2_send)
    drain(solved.at[:, pl.ds(0, (n_col - 1) * east_local), :], z2_send)


def finish_kernel(forcing, gathered, spread_r, out_hbm, result, sems):
    levels, east_local, north_local = result.shape
    modes = gathered.shape[0]

    def out_copy(a):
        rows = pl.ds(pl.multiple_of(a * PAIR, PAIR), PAIR)
        return pltpu.make_async_copy(result.at[:, rows, :], out_hbm.at[:, rows, :], sems.at[a])

    def finish(a, carry):
        rows = pl.ds(pl.multiple_of(a * PAIR, PAIR), PAIR)
        field = gathered[:, rows, :].astype(F32)
        halves = []
        for s in range(2):
            part = field[:, s * SUB : (s + 1) * SUB, :].reshape(modes * SUB, north_local)
            got = forcing[2 * a + s] + jnp.dot(
                spread_r[...], part.astype(BF16), preferred_element_type=F32
            )
            halves.append(got.reshape(levels, SUB, north_local))
        result[:, rows, :] = jnp.concatenate(halves, axis=1).astype(BF16)
        out_copy(a).start()
        return carry

    units = east_local // PAIR
    lax.fori_loop(0, units, finish, 0)
    for a in range(units):
        out_copy(a).wait()


def local(
    n_row, n_col,
    potential_temp, humidity, absorb, solar_flux, emission, sunlit, project, restore,
    east_basis, north_basis, east_weight, north_weight, east_eigen, north_eigen, coupling,
):
    levels, east_local, north_local = potential_temp.shape
    modes = project.shape[0]
    nx, ny = east_basis.shape[0], north_basis.shape[0]
    block = modes // n_col
    east_part = nx // n_row
    parts = part_units(east_local // PAIR)
    hbm = pl.BlockSpec(memory_space=pl.ANY)
    smem = pl.BlockSpec(memory_space=pltpu.SMEM)
    vmem = pl.BlockSpec(memory_space=pltpu.VMEM)
    dma = pltpu.SemaphoreType.DMA
    grid_lines = (block, nx, north_local)
    held = pl.pallas_call(
        functools.partial(kernel, n_row, n_col, parts),
        out_shape=(
            pltpu.VMEM((east_local // SUB, levels * SUB, north_local), F32),
            pltpu.VMEM((modes, east_local, north_local), BF16),
            pltpu.VMEM((levels * SUB, modes * SUB), BF16),
        ),
        in_specs=[
            hbm, hbm, smem, smem, smem, smem, vmem, vmem,
            hbm, hbm, vmem, vmem, vmem, vmem, smem,
        ],
        out_specs=(vmem, vmem, vmem),
        scratch_shapes=[
            pltpu.VMEM(potential_temp.shape, BF16),
            pltpu.VMEM(humidity.shape, BF16),
            pltpu.VMEM((nx, nx), BF16),
            pltpu.VMEM((ny, ny), BF16),
            pltpu.VMEM((nx, nx), BF16),
            pltpu.VMEM((modes * SUB, levels * SUB), BF16),
            pltpu.VMEM((east_part, 128), F32),
            pltpu.VMEM((modes, east_local, north_local), BF16),
            pltpu.VMEM(grid_lines, BF16),
            pltpu.VMEM((block, n_row, east_part, north_local), BF16),
            pltpu.VMEM((block, n_row, east_part, north_local), BF16),
            pltpu.VMEM((block, n_row, east_part, north_local), BF16),
            pltpu.VMEM(grid_lines, BF16),
            pltpu.VMEM(grid_lines, BF16),
            dma((2, len(parts))),
            dma((2,)),
            dma(()),
            dma((block + 1,)),
            dma(()),
            dma((block,)),
            dma(()),
            dma((block,)),
            dma(()),
            dma(()),
        ],
        compiler_params=pltpu.CompilerParams(
            collective_id=0, has_side_effects=True, vmem_limit_bytes=44 * 1024 * 1024
        ),
        name="semi_implicit_step",
    )(
        potential_temp, humidity, absorb, solar_flux, emission, sunlit, project, restore.T,
        east_basis, north_basis,
        east_weight.reshape(1, nx),
        north_weight.reshape(1, ny),
        east_eigen.reshape(1, nx),
        north_eigen.reshape(1, ny),
        coupling,
    )
    return pl.pallas_call(
        finish_kernel,
        out_shape=jax.ShapeDtypeStruct(potential_temp.shape, BF16),
        in_specs=[vmem, vmem, vmem],
        out_specs=hbm,
        scratch_shapes=[
            pltpu.VMEM(potential_temp.shape, BF16),
            dma((east_local // PAIR,)),
        ],
        compiler_params=pltpu.CompilerParams(vmem_limit_bytes=8 * 1024 * 1024),
        name="restore_levels",
    )(*held)


def solution(mesh):
    split = P(None, "col", "row")
    return jax.shard_map(
        functools.partial(local, mesh.shape["row"], mesh.shape["col"]),
        mesh=mesh,
        in_specs=(split, split) + (P(),) * 13,
        out_specs=split,
        check_vma=False,
    )
```

```python
import functools
import math

import jax
import jax.numpy as jnp
from jax import lax
from jax.experimental import pallas as pl
from jax.experimental.pallas import tpu as pltpu
from jax.sharding import PartitionSpec as P

SUB = 8
PAIR = 16
MESH = pl.DeviceIdType.MESH
F32 = jnp.float32
BF16 = jnp.bfloat16
SIZES = (1, 2, 2, 3)
EARLY = 4
SCHED = (("y", 1), ("f", 0), ("b", 1))


def spread(matrix):
    rows, cols = matrix.shape
    tall = (
        lax.broadcasted_iota(jnp.int32, (rows * SUB, rows), 0) // SUB
        == lax.broadcasted_iota(jnp.int32, (rows * SUB, rows), 1)
    ).astype(F32).astype(BF16)
    wide = (
        lax.broadcasted_iota(jnp.int32, (cols, cols * SUB), 1) // SUB
        == lax.broadcasted_iota(jnp.int32, (cols, cols * SUB), 0)
    ).astype(F32).astype(BF16)
    half = jnp.dot(tall, matrix.astype(BF16), preferred_element_type=F32).astype(BF16)
    full = jnp.dot(half, wide, preferred_element_type=F32)
    shape = (rows * SUB, cols * SUB)
    keep = (
        lax.broadcasted_iota(jnp.int32, shape, 0) % SUB
        == lax.broadcasted_iota(jnp.int32, shape, 1) % SUB
    )
    return jnp.where(keep, full, 0.0).astype(BF16)


def own_block(row_ref, index, count):
    width = row_ref.shape[1] // count
    found = row_ref[:, :width]
    for i in range(1, count):
        found = jnp.where(index == i, row_ref[:, i * width : (i + 1) * width], found)
    return found


def part_units(units):
    sizes = []
    for size in SIZES:
        if sum(sizes) < units:
            sizes.append(min(size, units - sum(sizes)))
    sizes += [1] * (units - sum(sizes))
    return tuple(sizes)


def early_modes(part, block):
    return min(block, EARLY if part == 0 else 1)


def partner(place, d, size):
    return lax.rem(place + d, size)


def far_first(size):
    return sorted(range(1, size), key=lambda d: abs(d - size // 2))


def kernel(
    n_row, n_col, parts,
    temp_hbm, hum_hbm, absorb, solar, emission, sunlit, project, restore,
    east_hbm, north_hbm, east_weight, north_weight, east_eigen, north_eigen, coupling,
    forcing, gathered, spread_r,
    temp, hum, east, north, east_t, spread_p, roots,
    modal, lines, moved, turned, back, joined, solved,
    in_sem, basis_sem,
    z1_send, z1_recv, y1_send, y1_recv, y2_send, y2_recv, z2_send, z2_recv,
):
    levels, east_local, north_local = temp.shape
    modes = project.shape[0]
    bands = absorb.shape[0]
    block = modes // n_col
    nx = east.shape[0]
    ny = north.shape[0]
    east_part = nx // n_row
    starts = [sum(parts[:p]) for p in range(len(parts))]
    r = lax.axis_index("row")
    c = lax.axis_index("col")

    barrier = pltpu.get_barrier_semaphore()
    for d in range(1, n_col):
        pl.semaphore_signal(
            barrier, inc=1, device_id=(r, lax.rem(c + d, n_col)), device_id_type=MESH
        )
    for d in range(1, n_row):
        pl.semaphore_signal(
            barrier, inc=1, device_id=(lax.rem(r + d, n_row), c), device_id_type=MESH
        )

    def drain(ref, sem):
        pltpu.make_async_copy(ref, ref, sem).wait()

    def fetch(part):
        rows = pl.ds(starts[part] * PAIR, parts[part] * PAIR)
        return (
            pltpu.make_async_copy(
                temp_hbm.at[:, rows, :], temp.at[:, rows, :], in_sem.at[0, part]
            ),
            pltpu.make_async_copy(
                hum_hbm.at[:, rows, :], hum.at[:, rows, :], in_sem.at[1, part]
            ),
        )

    fetches = [fetch(part) for part in range(len(parts))]
    for pair in fetches:
        for copy in pair:
            copy.start()
    get_east = pltpu.make_async_copy(east_hbm, east, basis_sem.at[0])
    get_north = pltpu.make_async_copy(north_hbm, north, basis_sem.at[1])

    spread_p[...] = spread(project[...])

    lit = sunlit[r, c]
    width = min(128, north_local)
    emit = [emission[b] for b in range(bands)]
    emit_all = emit[0]
    for b in range(1, bands):
        emit_all = emit_all + emit[b]
    unroll = 8

    def radiate(a, carry):
        top = pl.multiple_of(a * PAIR, PAIR)
        for lane in range(north_local // width):
            lanes = slice(lane * width, (lane + 1) * width)
            place = (top + lax.broadcasted_iota(jnp.int32, (PAIR, width), 0)) * north_local + (
                lane * width + lax.broadcasted_iota(jnp.int32, (PAIR, width), 1)
            )
            mask = (place < lit).astype(F32)
            beams = tuple(solar[b] * mask for b in range(bands))
            total = beams[0]
            for b in range(1, bands):
                total = total + beams[b]

            def level_group(group, state):
                beams, total = state
                for step in range(unroll):
                    level = group * unroll + step
                    t = temp[level, pl.ds(top, PAIR), lanes].astype(F32)
                    h = hum[level, pl.ds(top, PAIR), lanes].astype(F32)
                    new_beams = []
                    lower = None
                    glow = None
                    for b in range(bands):
                        passed = jnp.exp2(h * (absorb[b, level] * (-math.log2(math.e))))
                        beam = beams[b] * passed
                        new_beams.append(beam)
                        lower = beam if lower is None else lower + beam
                        part = passed * emit[b]
                        glow = part if glow is None else glow + part
                    value = (t + (total - lower)) - (emit_all - glow) * t
                    beams, total = tuple(new_beams), lower
                    at = pl.ds(pl.multiple_of(level * SUB, SUB), SUB)
                    forcing[2 * a, at, lanes] = value[:SUB]
                    forcing[2 * a + 1, at, lanes] = value[SUB:]
                return beams, total

            lax.fori_loop(0, levels // unroll, level_group, (beams, total))
        halves = []
        for s in range(2):
            got = jnp.dot(
                spread_p[...], forcing[2 * a + s].astype(BF16), preferred_element_type=F32
            )
            halves.append(got.reshape(modes, SUB, north_local))
        modal[:, pl.ds(top, PAIR), :] = jnp.concatenate(halves, axis=1).astype(BF16)
        return carry

    early = [early_modes(part, block) for part in range(len(parts))]
    late = {}
    for k in range(1, block):
        sent = sum(parts[p] for p in range(len(parts)) if early[p] > k) * PAIR
        if sent < east_local:
            late[k] = sent

    def z1_copy(d, group, first, count, start, rows):
        to = partner(c, d, n_col)
        return pltpu.make_async_remote_copy(
            src_ref=modal.at[pl.ds(to * block + first, count), pl.ds(start, rows), :],
            dst_ref=lines.at[
                pl.ds(first, count), pl.ds(pl.multiple_of(c * east_local + start, PAIR), rows), :
            ],
            send_sem=z1_send,
            recv_sem=z1_recv.at[group],
            device_id=(r, to),
            device_id_type=MESH,
        )

    def z1_early(part, d):
        group = block if early[part] > 1 else 0
        return z1_copy(d, group, 0, early[part], starts[part] * PAIR, parts[part] * PAIR)

    def z1_late(k, d):
        return z1_copy(d, k, k, 1, late[k], east_local - late[k])

    def z1_own(k):
        lines[k, pl.ds(pl.multiple_of(c * east_local, PAIR), east_local), :] = modal[c * block + k]

    order_col = far_first(n_col)
    order_row = far_first(n_row)
    for part in range(len(parts)):
        for copy in fetches[part]:
            copy.wait()
        if part == len(parts) - 1:
            get_east.start()
            get_north.start()
        lax.fori_loop(starts[part], starts[part] + parts[part], radiate, 0)
        if part == 0:
            pl.semaphore_wait(barrier, n_col - 1 + n_row - 1)
        for d in order_col:
            z1_early(part, d).start()
    for k in late:
        for d in order_col:
            z1_late(k, d).start()

    spread_r[...] = spread(jnp.transpose(restore[...]))

    def take_modal(a, carry):
        rows = pl.ds(pl.multiple_of(a * PAIR, PAIR), PAIR)
        field = modal[:, rows, :].astype(F32)
        for s in range(2):
            part = field[:, s * SUB : (s + 1) * SUB, :].reshape(modes * SUB, north_local)
            forcing[2 * a + s] -= jnp.dot(
                spread_r[...], part.astype(BF16), preferred_element_type=F32
            )
        return carry

    lax.fori_loop(0, east_local // PAIR, take_modal, 0)
    get_east.wait()

    turn = min(128, nx)

    def transpose_block(q, carry):
        at = pl.multiple_of(q * turn, turn)
        piece = jnp.transpose(east[pl.ds(at, turn), :].astype(F32))
        east_t[:, pl.ds(at, turn)] = (piece * east_weight[:, pl.ds(at, turn)]).astype(BF16)
        return carry

    lax.fori_loop(0, nx // turn, transpose_block, 0)
    roots[...] = jnp.transpose(
        jnp.broadcast_to(own_block(east_eigen, r, n_row), (128, east_part))
    )
    weight = own_block(north_weight, r, n_row)
    get_north.wait()

    def y1_copy(k, d):
        return pltpu.make_async_remote_copy(
            src_ref=moved.at[k, d],
            dst_ref=turned.at[k, r],
            send_sem=y1_send,
            recv_sem=y1_recv.at[k],
            device_id=(lax.rem(r + d, n_row), c),
            device_id_type=MESH,
        )

    def y2_copy(k, d):
        return pltpu.make_async_remote_copy(
            src_ref=back.at[k, d],
            dst_ref=joined.at[k, pl.ds(pl.multiple_of(r * east_part, PAIR), east_part), :],
            send_sem=y2_send,
            recv_sem=y2_recv.at[k],
            device_id=(lax.rem(r + d, n_row), c),
            device_id_type=MESH,
        )

    def z2_copy(k, d):
        to = partner(c, d, n_col)
        return pltpu.make_async_remote_copy(
            src_ref=solved.at[k, pl.ds(pl.multiple_of(to * east_local, PAIR), east_local), :],
            dst_ref=gathered.at[c * block + k],
            send_sem=z2_send,
            recv_sem=z2_recv,
            device_id=(r, to),
            device_id_type=MESH,
        )

    def z2_own(k):
        gathered[c * block + k] = solved[
            k, pl.ds(pl.multiple_of(c * east_local, PAIR), east_local), :
        ]

    def x_forward(k):
        z1_own(k)

        @pl.when(k == 0)
        def _():
            for count in sorted(set(early)):
                rows = sum(parts[p] for p in range(len(parts)) if early[p] == count) * PAIR
                drain(
                    lines.at[pl.ds(0, count), pl.ds(0, (n_col - 1) * rows), :],
                    z1_recv.at[block if count > 1 else 0],
                )

        for later in late:

            @pl.when(k == later)
            def _():
                rows = (n_col - 1) * (east_local - late[later])
                drain(lines.at[later, pl.ds(0, rows), :], z1_recv.at[later])

        for d in order_row + [0]:
            to = lax.rem(r + d, n_row)
            got = jnp.dot(
                east_t[pl.ds(pl.multiple_of(to * east_part, PAIR), east_part), :],
                lines[k],
                preferred_element_type=F32,
            )
            got = (got * weight).astype(BF16)
            if d == 0:
                turned[k, r] = got
            else:
                moved[k, d] = got
                y1_copy(k, d).start()

    def y_both(k):
        drain(turned.at[k, pl.ds(0, n_row - 1)], y1_recv.at[k])
        total = None
        for source in range(n_row):
            term = jnp.dot(
                turned[k, source],
                north[source * north_local : (source + 1) * north_local, :],
                preferred_element_type=F32,
            )
            total = term if total is None else total + term
        side = roots[...]
        gravity = coupling[c * block + k]
        pieces = []
        for lane in range(ny // 128):
            lanes = slice(lane * 128, (lane + 1) * 128)
            divisor = 1.0 + gravity * (side + north_eigen[:, lanes])
            pieces.append((total[:, lanes] / divisor).astype(BF16))
        scaled = jnp.concatenate(pieces, axis=1)
        for d in order_row + [0]:
            to = lax.rem(r + d, n_row)
            got = lax.dot_general(
                scaled,
                north[pl.ds(pl.multiple_of(to * north_local, PAIR), north_local), :],
                (((1,), (1,)), ((), ())),
                preferred_element_type=F32,
            ).astype(BF16)
            if d == 0:
                joined[k, pl.ds(pl.multiple_of(r * east_part, PAIR), east_part), :] = got
            else:
                back[k, d] = got
                y2_copy(k, d).start()

    def x_back(k):
        drain(joined.at[k, pl.ds(0, (n_row - 1) * east_part), :], y2_recv.at[k])
        rows = min(256, nx)
        for q in range(nx // rows):
            solved[k, q * rows : (q + 1) * rows, :] = jnp.dot(
                east[q * rows : (q + 1) * rows, :], joined[k], preferred_element_type=F32
            ).astype(BF16)

        for d in order_col:
            z2_copy(k, d).start()
        z2_own(k)

    run = {"f": x_forward, "y": y_both, "b": x_back}

    def stage(t, carry):
        for name, lag in SCHED:

            @pl.when(jnp.logical_and(t >= lag, t < block + lag))
            def _():
                run[name](t - lag)

        return carry

    lax.fori_loop(0, block + max(lag for _, lag in SCHED), stage, 0)

    drain(gathered.at[pl.ds(0, block * (n_col - 1))], z2_recv)
    drain(modal.at[pl.ds(0, block * (n_col - 1))], z1_send)
    drain(moved.at[:, pl.ds(0, n_row - 1)], y1_send)
    drain(back.at[:, pl.ds(0, n_row - 1)], y2_send)
    drain(solved.at[:, pl.ds(0, (n_col - 1) * east_local), :], z2_send)


def finish_kernel(forcing, gathered, spread_r, out_hbm, result, sems):
    levels, east_local, north_local = result.shape
    modes = gathered.shape[0]

    def out_copy(a):
        rows = pl.ds(pl.multiple_of(a * PAIR, PAIR), PAIR)
        return pltpu.make_async_copy(result.at[:, rows, :], out_hbm.at[:, rows, :], sems.at[a])

    def finish(a, carry):
        rows = pl.ds(pl.multiple_of(a * PAIR, PAIR), PAIR)
        field = gathered[:, rows, :].astype(F32)
        halves = []
        for s in range(2):
            part = field[:, s * SUB : (s + 1) * SUB, :].reshape(modes * SUB, north_local)
            got = forcing[2 * a + s] + jnp.dot(
                spread_r[...], part.astype(BF16), preferred_element_type=F32
            )
            halves.append(got.reshape(levels, SUB, north_local))
        result[:, rows, :] = jnp.concatenate(halves, axis=1).astype(BF16)
        out_copy(a).start()
        return carry

    units = east_local // PAIR
    lax.fori_loop(0, units, finish, 0, unroll=True)
    for a in range(units):
        out_copy(a).wait()


def local(
    n_row, n_col,
    potential_temp, humidity, absorb, solar_flux, emission, sunlit, project, restore,
    east_basis, north_basis, east_weight, north_weight, east_eigen, north_eigen, coupling,
):
    levels, east_local, north_local = potential_temp.shape
    modes = project.shape[0]
    nx, ny = east_basis.shape[0], north_basis.shape[0]
    block = modes // n_col
    east_part = nx // n_row
    parts = part_units(east_local // PAIR)
    hbm = pl.BlockSpec(memory_space=pl.ANY)
    smem = pl.BlockSpec(memory_space=pltpu.SMEM)
    vmem = pl.BlockSpec(memory_space=pltpu.VMEM)
    dma = pltpu.SemaphoreType.DMA
    grid_lines = (block, nx, north_local)
    held = pl.pallas_call(
        functools.partial(kernel, n_row, n_col, parts),
        out_shape=(
            pltpu.VMEM((east_local // SUB, levels * SUB, north_local), F32),
            pltpu.VMEM((modes, east_local, north_local), BF16),
            pltpu.VMEM((levels * SUB, modes * SUB), BF16),
        ),
        in_specs=[
            hbm, hbm, smem, smem, smem, smem, vmem, vmem,
            hbm, hbm, vmem, vmem, vmem, vmem, smem,
        ],
        out_specs=(vmem, vmem, vmem),
        scratch_shapes=[
            pltpu.VMEM(potential_temp.shape, BF16),
            pltpu.VMEM(humidity.shape, BF16),
            pltpu.VMEM((nx, nx), BF16),
            pltpu.VMEM((ny, ny), BF16),
            pltpu.VMEM((nx, nx), BF16),
            pltpu.VMEM((modes * SUB, levels * SUB), BF16),
            pltpu.VMEM((east_part, 128), F32),
            pltpu.VMEM((modes, east_local, north_local), BF16),
            pltpu.VMEM(grid_lines, BF16),
            pltpu.VMEM((block, n_row, east_part, north_local), BF16),
            pltpu.VMEM((block, n_row, east_part, north_local), BF16),
            pltpu.VMEM((block, n_row, east_part, north_local), BF16),
            pltpu.VMEM(grid_lines, BF16),
            pltpu.VMEM(grid_lines, BF16),
            dma((2, len(parts))),
            dma((2,)),
            dma(()),
            dma((block + 1,)),
            dma(()),
            dma((block,)),
            dma(()),
            dma((block,)),
            dma(()),
            dma(()),
        ],
        compiler_params=pltpu.CompilerParams(
            collective_id=0, has_side_effects=True, vmem_limit_bytes=44 * 1024 * 1024
        ),
        name="semi_implicit_step",
    )(
        potential_temp, humidity, absorb, solar_flux, emission, sunlit, project, restore.T,
        east_basis, north_basis,
        east_weight.reshape(1, nx),
        north_weight.reshape(1, ny),
        east_eigen.reshape(1, nx),
        north_eigen.reshape(1, ny),
        coupling,
    )
    return pl.pallas_call(
        finish_kernel,
        out_shape=jax.ShapeDtypeStruct(potential_temp.shape, BF16),
        in_specs=[vmem, vmem, vmem],
        out_specs=hbm,
        scratch_shapes=[
            pltpu.VMEM(potential_temp.shape, BF16),
            dma((east_local // PAIR,)),
        ],
        compiler_params=pltpu.CompilerParams(vmem_limit_bytes=8 * 1024 * 1024),
        name="restore_levels",
    )(*held)


def solution(mesh):
    split = P(None, "col", "row")
    return jax.shard_map(
        functools.partial(local, mesh.shape["row"], mesh.shape["col"]),
        mesh=mesh,
        in_specs=(split, split) + (P(),) * 13,
        out_specs=split,
        check_vma=False,
    )
```
